256 devices in a mesh: dp: 32 (over y, x, core), vocab: 8 (over z).
Axes of the slice: x: 4, y: 4, z: 8, core: 2. Of those that a mesh axis runs over, the one named last changes fastest.
Arguments:
- hidden_states: float32 [24576, 2048], P('dp'), may hold values from -8 to 8
- norm_gain: float32 [2048], replicated, may hold values from 0.5 to 1.5
- head_weight: bfloat16 [32768, 2048], P(('vocab', 'dp')), may hold values from -2 to 2
- target_ids: int32 [24576], P('dp'), may hold values from 0 to 32767
- lengths: int32 [32], P('dp'), may hold values from 1 to 768, as said below
Outputs:
- log_probs: float32 [24576], P('dp')
- entropies: float32 [24576], P('dp')
The draws below stay inside these ranges and needn't reach their ends.
Inputs may be any that keep to these rules, and one draw needn't show every extreme that they name: `lengths`: live tokens of a sequence; some sequence fills all 768 slots.
All inputs are finite; a program needn't handle non-finite values.
Results may differ from the reference program's by a relative error of at most 0.0015.
Values may be sent and summed in bfloat16 or wider, within the bound.
No kernel may reach another device: no remote copies, remote signals or barrier semaphores. Data moves between devices by JAX's collectives and lax.ppermute only.
A program may use at most 128 MiB of HBM per device.

```python
import jax
import jax.numpy as jnp
from jax import lax

D = 2048
VOCAB = 32768
LEN = 768
SEQS = 32
TOKENS = 24576


def planted_rows(key):
    order = jax.random.permutation(jax.random.fold_in(key, 71), VOCAB)
    chosen_rows = order[:8]
    partner_rows = order[8:16]
    seq_order = jax.random.permutation(jax.random.fold_in(key, 73), SEQS)
    slot_rows = seq_order[:8] * LEN
    signs = jnp.where(jax.random.bernoulli(jax.random.fold_in(key, 74), 0.5, (8, D)), 1.0, -1.0)
    strength = 120.0 + 200.0 * jnp.arange(8, dtype=jnp.float32) / 7.0
    return (chosen_rows, partner_rows, slot_rows, signs, strength)


def draw_head_weight(key, part):
    values = jnp.clip(jax.random.normal(jax.random.fold_in(key, 11), (VOCAB, D), jnp.float32), -6.0, 6.0) * 0.07
    chosen_rows, partner_rows, slot_rows, signs, strength = planted_rows(key)
    values = values.at[chosen_rows].set(signs * (strength[:, None] / D))
    values = values.at[partner_rows].set(signs * ((strength[:, None] - 2.0) / D))
    return values.astype(jnp.bfloat16)


def draw_hidden_states(key, part):
    values = jnp.clip(jax.random.normal(jax.random.fold_in(key, 12), (TOKENS, D), jnp.float32), -6.0, 6.0)
    chosen_rows, partner_rows, slot_rows, signs, strength = planted_rows(key)
    return values.at[slot_rows].set(signs)


def draw_lengths(key, part):
    values = jax.random.randint(jax.random.fold_in(key, 31), (SEQS,), 1, LEN + 1)
    filled = jax.random.randint(jax.random.fold_in(key, 32), (), 0, SEQS)
    return values.at[filled].set(LEN).astype(jnp.int32)


def place_ends(result, own_key, low, high):
    longest = result.shape.index(max(result.shape))
    spots = []
    for shift in (0, 1):
        where = [jax.random.randint(jax.random.fold_in(own_key, axis), (), 0, length) for axis, length in enumerate(result.shape)]
        where[longest] = (where[longest] + shift) % result.shape[longest]
        spots.append(tuple(where))
    return result.at[spots[0]].set(low).at[spots[1]].set(high)


def setup_inputs(seed: int = 0) -> dict:
    key_of = jax.random.split(jax.random.key(seed), 6)
    hidden_states = draw_hidden_states(jax.random.fold_in(key_of[5], 71), 0)
    norm_gain = jnp.clip(1.0 + 0.1 * jax.random.normal(key_of[1], (D,), jnp.float32), 0.5, 1.5)
    head_weight = draw_head_weight(jax.random.fold_in(key_of[5], 71), 0)
    target_ids = place_ends(jax.random.randint(key_of[3], (TOKENS,), 0, VOCAB), jax.random.fold_in(key_of[3], 1), 0, VOCAB - 1).astype(jnp.int32)
    lengths = draw_lengths(jax.random.fold_in(key_of[5], 71), 0)
    return dict(hidden_states=hidden_states, norm_gain=norm_gain, head_weight=head_weight, target_ids=target_ids, lengths=lengths)


epsilon = 1e-05

def reference(hidden_states, norm_gain, head_weight, target_ids, lengths):
    states = hidden_states.reshape(SEQS, LEN, D)
    goals = target_ids.reshape(SEQS, LEN)

    def score_sequence(packed):
        seq_states, seq_goals = packed
        scale = lax.rsqrt(lax.optimization_barrier(jnp.mean(seq_states * seq_states, axis=1, keepdims=True)) + epsilon)
        normed = (seq_states * scale * norm_gain).astype(jnp.bfloat16)
        logits = lax.dot_general(normed, head_weight, (((1,), (1,)), ((), ())), preferred_element_type=jnp.float32)
        maxima = lax.optimization_barrier(jnp.max(logits, axis=1))
        weights = jnp.exp(logits - maxima[:, None])
        totals = lax.optimization_barrier(jnp.sum(weights, axis=1))
        tilted = lax.optimization_barrier(jnp.sum(weights * logits, axis=1))
        log_total = maxima + jnp.log(totals)
        picked = jnp.take_along_axis(logits, seq_goals[:, None].astype(jnp.int32), axis=1)[:, 0]
        return (picked - log_total, log_total - tilted / totals)
    chosen, spread = lax.map(score_sequence, (states, goals))
    positions = jnp.arange(LEN, dtype=jnp.int32)
    live_mask = positions[None, :] < lengths[:, None]
    log_probs = jnp.where(live_mask, chosen, 0.0).reshape(TOKENS)
    entropies = jnp.where(live_mask, spread, 0.0).reshape(TOKENS)
    return (log_probs, entropies)
```

```python
import functools

import jax
import jax.numpy as jnp
from jax import lax
from jax.experimental import pallas as pl
from jax.experimental.pallas import tpu as pltpu
from jax.sharding import PartitionSpec as P

epsilon = 1e-05
lowest = -1e30


SIDE = 4
TOKEN_BLOCK = 256


def index_of(y, x, core):
    return ((y % SIDE) * SIDE + x % SIDE) * 2 + core


def shift(value, dy, dx):
    pairs = [
        (index_of(y, x, c), index_of(y + dy, x + dx, c))
        for y in range(SIDE)
        for x in range(SIDE)
        for c in range(2)
    ]
    return lax.ppermute(value, "dp", pairs)


def swap_cores(value):
    return lax.ppermute(value, "dp", [(i, i ^ 1) for i in range(2 * SIDE * SIDE)])


def norm_kernel(h_ref, g_ref, o_ref):
    h = h_ref[...]
    scale = lax.rsqrt(jnp.mean(h * h, axis=1, keepdims=True) + epsilon)
    o_ref[...] = (h * scale * g_ref[...]).astype(jnp.bfloat16)


def normalize(hidden_states, norm_gain):
    rows, width = hidden_states.shape
    block = 128
    return pl.pallas_call(
        norm_kernel,
        grid=(rows // block,),
        in_specs=[
            pl.BlockSpec((block, width), lambda i: (i, 0)),
            pl.BlockSpec((1, width), lambda i: (0, 0)),
        ],
        out_specs=pl.BlockSpec((block, width), lambda i: (i, 0)),
        out_shape=jax.ShapeDtypeStruct((rows, width), jnp.bfloat16),
        cost_estimate=pl.CostEstimate(flops=4 * rows * width, bytes_accessed=6 * rows * width, transcendentals=rows),
        name="normalize",
    )(hidden_states, norm_gain.reshape(1, width))


def score_body(heights, spans, base_ref, x_ref, goal_ref, prev_ref, refs):
    count = len(heights)
    pieces, out_ref, rows_ref = refs[:count], refs[count], refs[count + 1]

    @pl.when(pl.program_id(0) == 0)
    def _():
        at = 0
        for piece, height in zip(pieces, heights):
            rows_ref[at : at + height, :] = piece[...]
            at += height

    logits = lax.dot_general(
        rows_ref[...], x_ref[...], (((1,), (1,)), ((), ())), preferred_element_type=jnp.float32
    )
    prev = prev_ref[...]
    old = prev[0:1]
    highest = jnp.maximum(old, jnp.max(logits, axis=0, keepdims=True))
    weights = jnp.exp(logits - highest)
    factor = jnp.exp(old - highest)
    out_ref[0:1, :] = highest
    out_ref[1:2, :] = prev[1:2] * factor + jnp.sum(weights, axis=0, keepdims=True)
    out_ref[2:3, :] = prev[2:3] * factor + jnp.sum(weights * logits, axis=0, keepdims=True)
    goal = goal_ref[0:1, :]
    target = prev[3:4]
    at = 0
    for k, span in enumerate(spans):
        part = logits[at : at + span]
        line = lax.broadcasted_iota(jnp.int32, part.shape, 0)
        hit = line == goal - base_ref[k]
        target = target + jnp.sum(jnp.where(hit, part, 0.0), axis=0, keepdims=True)
        at += span
    out_ref[3:4, :] = target


def score_groups(tokens, goals, prev, values, sizes, bases):
    flat = tuple(s for group in sizes for s in group)
    count = sum(flat)
    slots, width = tokens.shape
    block = TOKEN_BLOCK
    whole = lambda i, b: (0, 0)
    heights = tuple(v.shape[0] for v in values)

    def body(base_ref, x_ref, goal_ref, prev_ref, *refs):
        score_body(heights, flat, base_ref, x_ref, goal_ref, prev_ref, refs)

    return pl.pallas_call(
        body,
        grid_spec=pltpu.PrefetchScalarGridSpec(
            num_scalar_prefetch=1,
            grid=(slots // block,),
            in_specs=[
                pl.BlockSpec((block, width), lambda i, b: (i, 0)),
                pl.BlockSpec((1, block), lambda i, b: (0, i)),
                pl.BlockSpec((4, block), lambda i, b: (0, i)),
            ]
            + [pl.BlockSpec((h, width), whole) for h in heights],
            out_specs=pl.BlockSpec((4, block), lambda i, b: (0, i)),
            scratch_shapes=[pltpu.VMEM((count, width), jnp.bfloat16)],
        ),
        out_shape=jax.ShapeDtypeStruct((4, slots), jnp.float32),
        cost_estimate=pl.CostEstimate(
            flops=2 * count * slots * width,
            bytes_accessed=2 * (count + slots) * width,
            transcendentals=count * slots,
        ),
        name="score",
    )(jnp.stack(bases), tokens, goals, prev, *values)


def merge(parts):
    highest = functools.reduce(jnp.maximum, [p[0] for p in parts])
    factors = [jnp.exp(p[0] - highest) for p in parts]
    totals = sum(p[1] * f for p, f in zip(parts, factors))
    tilted = sum(p[2] * f for p, f in zip(parts, factors))
    target = sum(p[3] for p in parts)
    return highest, totals, tilted, target


def on_device(hidden_states, norm_gain, head_weight, target_ids, lengths):
    row_count = hidden_states.shape[0]
    chunk = head_weight.shape[0]
    half, quarter = chunk // 2, chunk // 4
    place = lax.axis_index("dp")
    core, x, y = place % 2, (place // 2) % SIDE, place // (2 * SIDE)
    first_row = lax.axis_index("vocab") * (chunk * lax.axis_size("dp"))

    def base(dy, dx, offset):
        owner = (((y + dy + SIDE) % SIDE) * SIDE + (x + dx + SIDE) % SIDE) * 2 + core
        return first_row + owner * chunk + offset

    held = {}

    def put(value, *names):
        at = 0
        for kind, dy, dx, lo, hi in names:
            held[kind, dy, dx, lo] = (value[at : at + hi - lo], base(dy, dx, lo + (half if kind == "b" else 0)))
            at += hi - lo

    def get(kind, dy, dx, lo=0, hi=half):
        return held[kind, dy, dx, 0][0][lo:hi]

    q = quarter
    cat = lambda *v: jnp.concatenate(v, axis=0)
    own = head_weight
    put(own, ("a", 0, 0, 0, half), ("b", 0, 0, 0, half))
    w_left, w_right = shift(own, 0, 1), shift(own, 0, -1)
    w_down, w_up = shift(own, 1, 0), shift(own, -1, 0)
    put(w_left, ("a", 0, -1, 0, half), ("b", 0, -1, 0, half))
    put(w_right, ("a", 0, 1, 0, half), ("b", 0, 1, 0, half))
    put(w_down, ("a", -1, 0, 0, half), ("b", -1, 0, 0, half))
    put(w_up, ("a", 1, 0, 0, half), ("b", 1, 0, 0, half))

    normed = normalize(hidden_states, norm_gain)
    tokens = cat(normed, swap_cores(normed))
    goals = jnp.concatenate([target_ids, swap_cores(target_ids)]).reshape(1, 2 * row_count)

    one_xp = shift(cat(get("b", -1, 0), get("b", 1, 0), get("a", 0, -1, 0, q), get("b", 0, -1, 0, q)), 0, 1)
    one_xm = shift(cat(get("b", -1, 0), get("b", 1, 0), get("a", 0, 1, q), get("b", 0, 1, q)), 0, -1)
    one_yp = shift(cat(get("a", 0, -1), get("a", 0, 1), get("b", -1, 0, 0, q), get("a", -1, 0, 0, q)), 1, 0)
    one_ym = shift(cat(get("a", 0, -1), get("a", 0, 1), get("b", 1, 0, q), get("a", 1, 0, q)), -1, 0)
    initial = jnp.concatenate(
        [jnp.full((1, 2 * row_count), lowest, jnp.float32), jnp.zeros((3, 2 * row_count), jnp.float32)]
    )
    near = [own, w_left, w_right, w_down, w_up]
    near_bases = [base(0, 0, 0), base(0, -1, 0), base(0, 1, 0), base(-1, 0, 0), base(1, 0, 0)]
    stats = score_groups(tokens, goals, initial, near, [[chunk]] * len(near), near_bases)

    a2 = cat(one_xp[2 * half : 2 * half + q], one_xm[2 * half : 2 * half + q])
    b2 = cat(one_yp[2 * half : 2 * half + q], one_ym[2 * half : 2 * half + q])
    two_yp = shift(cat(a2, one_yp[:q], one_yp[half : half + q]), 1, 0)
    two_ym = shift(cat(a2, one_ym[q:half], one_ym[half + q : 2 * half]), -1, 0)
    two_xp = shift(cat(b2, one_xp[:q], one_xp[half : half + q]), 0, 1)
    two_xm = shift(cat(b2, one_xm[q:half], one_xm[half + q : 2 * half]), 0, -1)

    def spans_of(value, names):
        pieces, bases, at = [], [], 0
        for kind, dy, dx, lo, size in names:
            pieces.append(size)
            bases.append(base(dy, dx, lo + (half if kind == "b" else 0)))
            at += size
        return value, pieces, bases

    def score_sent(stats, sent):
        values, sizes, bases = [], [], []
        for value, names in sent:
            _, s, b = spans_of(value, names)
            values.append(value)
            sizes.append(s)
            bases.extend(b)
        return score_groups(tokens, goals, stats, values, sizes, bases)

    stats = score_sent(
        stats,
        [
            (one_xp, [("b", -1, -1, 0, half), ("b", 1, -1, 0, half), ("a", 0, 2, 0, q), ("b", 0, 2, 0, q)]),
            (one_xm, [("b", -1, 1, 0, half), ("b", 1, 1, 0, half), ("a", 0, 2, q, q), ("b", 0, 2, q, q)]),
            (one_yp, [("a", -1, -1, 0, half), ("a", -1, 1, 0, half), ("b", 2, 0, 0, q), ("a", 2, 0, 0, q)]),
            (one_ym, [("a", 1, -1, 0, half), ("a", 1, 1, 0, half), ("b", 2, 0, q, q), ("a", 2, 0, q, q)]),
        ],
    )
    three_yp, three_ym = shift(two_yp[:q], 1, 0), shift(two_ym[q:half], -1, 0)
    three_xp, three_xm = shift(two_xp[:q], 0, 1), shift(two_xm[q:half], 0, -1)
    stats = score_sent(
        stats,
        [
            (two_yp, [("a", -1, 2, 0, half), ("a", 2, -1, 0, q), ("a", 2, 1, 0, q)]),
            (two_ym, [("a", 1, 2, 0, half), ("a", 2, -1, q, q), ("a", 2, 1, q, q)]),
            (two_xp, [("b", 2, -1, 0, half), ("b", -1, 2, 0, q), ("b", 1, 2, 0, q)]),
            (two_xm, [("b", 2, 1, 0, half), ("b", -1, 2, q, q), ("b", 1, 2, q, q)]),
        ],
    )
    stats = score_sent(
        stats,
        [
            (three_yp, [("a", 2, 2, 0, q)]),
            (three_ym, [("a", 2, 2, q, q)]),
            (three_xp, [("b", 2, 2, 0, q)]),
            (three_xm, [("b", 2, 2, q, q)]),
        ],
    )

    other = swap_cores(stats[:, row_count:])
    mine = jnp.stack(merge([stats[:, :row_count], other]))
    depth = lax.axis_size("vocab")
    forth = [(i, (i + 1) % depth) for i in range(depth)]
    back = [(i, (i - 1) % depth) for i in range(depth)]
    parts = [mine]
    up = down = mine
    for step in range(depth // 2):
        up = lax.ppermute(up, "vocab", forth)
        parts.append(up)
        if step < depth // 2 - 1:
            down = lax.ppermute(down, "vocab", back)
            parts.append(down)
    highest, totals, tilted, target = merge(parts)
    log_total = highest + jnp.log(totals)
    live = jnp.arange(row_count, dtype=jnp.int32) < lengths[0]
    log_probs = jnp.where(live, target - log_total, 0.0)
    entropies = jnp.where(live, log_total - tilted / totals, 0.0)
    return (log_probs, entropies)


def solution(mesh):
    in_specs = (P("dp", None), P(), P(("vocab", "dp"), None), P("dp"), P("dp"))
    out_specs = (P("dp"), P("dp"))
    return jax.shard_map(
        on_device, mesh=mesh, in_specs=in_specs, out_specs=out_specs, check_vma=False
    )
```

```python
import functools

import jax
import jax.numpy as jnp
from jax import lax
from jax.experimental import pallas as pl
from jax.experimental.pallas import tpu as pltpu
from jax.sharding import PartitionSpec as P


epsilon = 1e-05
lowest = -1e30


SIDE = 4
BLOCK = 256


def index_of(y, x, core):
    return ((y % SIDE) * SIDE + x % SIDE) * 2 + core


def shift(value, dy, dx):
    pairs = [
        (index_of(y, x, c), index_of(y + dy, x + dx, c))
        for y in range(SIDE)
        for x in range(SIDE)
        for c in range(2)
    ]
    return lax.ppermute(value, "dp", pairs)


def swap_cores(value):
    return lax.ppermute(value, "dp", [(i, i ^ 1) for i in range(2 * SIDE * SIDE)])


def norm_kernel(h_ref, g_ref, o_ref):
    h = h_ref[...]
    scale = lax.rsqrt(jnp.mean(h * h, axis=1, keepdims=True) + epsilon)
    o_ref[0] = (h * scale * g_ref[...]).astype(jnp.bfloat16).T


def normalize(hidden_states, norm_gain):
    rows, width = hidden_states.shape
    return pl.pallas_call(
        norm_kernel,
        grid=(rows // BLOCK,),
        in_specs=[
            pl.BlockSpec((BLOCK, width), lambda i: (i, 0)),
            pl.BlockSpec((1, width), lambda i: (0, 0)),
        ],
        out_specs=pl.BlockSpec((1, width, BLOCK), lambda i: (i, 0, 0)),
        out_shape=jax.ShapeDtypeStruct((rows // BLOCK, width, BLOCK), jnp.bfloat16),
        cost_estimate=pl.CostEstimate(flops=4 * rows * width, bytes_accessed=6 * rows * width, transcendentals=rows),
        name="normalize",
    )(hidden_states, norm_gain.reshape(1, width))


def score_kernel(heights, spans, chunk, last, place_ref, goal_ref, prev_ref, own_ref, other_ref, *refs):
    count = len(heights)
    pieces, refs = refs[:count], refs[count:]
    outs, refs = (refs[:2], refs[2:]) if last else (refs[:1], refs[1:])
    rows_ref, tokens_ref, rows_sem, tokens_sem = refs
    mine = own_ref.shape[0]
    blocks = 2 * mine

    at = 0
    row_copies = []
    for k, (piece, height) in enumerate(zip(pieces, heights)):
        row_copies.append(pltpu.make_async_copy(piece, rows_ref.at[pl.ds(at, height)], rows_sem.at[k]))
        at += height
    for copy in row_copies:
        copy.start()

    def fetch(source, block, slot):
        return pltpu.make_async_copy(source.at[block], tokens_ref.at[slot], tokens_sem.at[slot])

    fetch(own_ref, 0, 0).start()
    for copy in row_copies:
        copy.wait()
    first, y, x, core = place_ref[0], place_ref[1], place_ref[2], place_ref[3]
    bases = []
    for dy, dx, offset, _ in spans:
        owner = (((y + dy) & (SIDE - 1)) * SIDE + ((x + dx) & (SIDE - 1))) * 2 + core
        bases.append(first + owner * chunk + offset)

    def step(i, carry):
        slot = lax.rem(i, 2)
        after = i + 1

        @pl.when(after < mine)
        def _():
            fetch(own_ref, after, 1 - slot).start()

        @pl.when((after >= mine) & (after < blocks))
        def _():
            fetch(other_ref, after - mine, 1 - slot).start()

        fetch(own_ref, 0, slot).wait()
        logits = jnp.dot(rows_ref[...], tokens_ref[slot], preferred_element_type=jnp.float32)
        prev = prev_ref[i]
        old = prev[0:1]
        highest = jnp.maximum(old, jnp.max(logits, axis=0, keepdims=True))
        weights = jnp.exp(logits - highest)
        factor = jnp.exp(old - highest)
        totals = prev[1:2] * factor + jnp.sum(weights, axis=0, keepdims=True)
        tilted = prev[2:3] * factor + jnp.sum(weights * logits, axis=0, keepdims=True)
        goal = goal_ref[i]
        target = prev[3:4]
        at = 0
        for base, (_, _, _, span) in zip(bases, spans):
            part = logits[at : at + span]
            line = lax.broadcasted_iota(jnp.int32, part.shape, 0)
            target = target + jnp.sum(jnp.where(line == goal - base, part, 0.0), axis=0, keepdims=True)
            at += span

        def write(ref, block):
            ref[block, 0:1, :] = highest
            ref[block, 1:2, :] = totals
            ref[block, 2:3, :] = tilted
            ref[block, 3:4, :] = target

        if last:

            @pl.when(i < mine)
            def _():
                write(outs[0], i)

            @pl.when(i >= mine)
            def _():
                write(outs[1], i - mine)

        else:
            write(outs[0], i)
        return carry

    lax.fori_loop(0, blocks, step, 0)


def score(place, goals, prev, own, other, chunk, pieces, last=False):
    values = [value for value, _ in pieces]
    spans = tuple(span for _, names in pieces for span in names)
    heights = tuple(v.shape[0] for v in values)
    total, (mine, width, block) = sum(heights), own.shape
    slots = 2 * mine * block
    if last:
        out_shape = [jax.ShapeDtypeStruct((mine, 4, block), jnp.float32)] * 2
    else:
        out_shape = [jax.ShapeDtypeStruct((2 * mine, 4, block), jnp.float32)]
    anywhere = pl.BlockSpec(memory_space=pl.ANY)
    local = pl.BlockSpec(memory_space=pltpu.VMEM)
    return pl.pallas_call(
        functools.partial(score_kernel, heights, spans, chunk, last),
        in_specs=[pl.BlockSpec(memory_space=pltpu.SMEM), local, local, anywhere, anywhere]
        + [anywhere] * len(values),
        out_specs=[local] * len(out_shape),
        out_shape=out_shape,
        scratch_shapes=[
            pltpu.VMEM((total, width), jnp.bfloat16),
            pltpu.VMEM((2, width, block), jnp.bfloat16),
            pltpu.SemaphoreType.DMA((len(values),)),
            pltpu.SemaphoreType.DMA((2,)),
        ],
        compiler_params=pltpu.CompilerParams(vmem_limit_bytes=24 << 20),
        cost_estimate=pl.CostEstimate(
            flops=2 * total * slots * width,
            bytes_accessed=2 * (total + slots) * width,
            transcendentals=total * slots,
        ),
        name="score",
    )(place, goals, prev, own, other, *values)


def fold(parts):
    highest = functools.reduce(jnp.maximum, [p[:, 0:1] for p in parts])
    factors = [jnp.exp(p[:, 0:1] - highest) for p in parts]
    totals = sum(p[:, 1:2] * f for p, f in zip(parts, factors))
    tilted = sum(p[:, 2:3] * f for p, f in zip(parts, factors))
    target = sum(p[:, 3:4] for p in parts)
    return highest, totals, tilted, target


def merge_kernel(a_ref, b_ref, o_ref):
    for k, value in enumerate(fold([a_ref[...], b_ref[...]])):
        o_ref[:, k : k + 1, :] = value


def merge(a, b):
    return pl.pallas_call(merge_kernel, out_shape=jax.ShapeDtypeStruct(a.shape, a.dtype), name="merge")(a, b)


def finish_kernel(length_ref, *refs):
    parts, (log_probs_ref, entropies_ref) = refs[:-2], refs[-2:]
    highest, totals, tilted, target = fold([p[...] for p in parts])
    log_total = highest + jnp.log(totals)
    block = lax.broadcasted_iota(jnp.int32, highest.shape, 0)
    slot = lax.broadcasted_iota(jnp.int32, highest.shape, 2)
    live = block * highest.shape[2] + slot < length_ref[0]
    log_probs_ref[...] = jnp.where(live, target - log_total, 0.0)
    entropies_ref[...] = jnp.where(live, log_total - tilted / totals, 0.0)


def finish(lengths, parts):
    blocks, _, block = parts[0].shape
    local = pl.BlockSpec(memory_space=pltpu.VMEM)
    return pl.pallas_call(
        finish_kernel,
        in_specs=[pl.BlockSpec(memory_space=pltpu.SMEM)] + [local] * len(parts),
        out_specs=[local] * 2,
        out_shape=[jax.ShapeDtypeStruct((blocks, 1, block), jnp.float32)] * 2,
        name="finish",
    )(lengths, *parts)


def on_device(hidden_states, norm_gain, head_weight, target_ids, lengths):
    row_count = hidden_states.shape[0]
    chunk = head_weight.shape[0]
    h, q = chunk // 2, chunk // 4
    mine = row_count // BLOCK
    device = lax.axis_index("dp")
    core, x, y = device % 2, (device // 2) % SIDE, device // (2 * SIDE)
    first_row = lax.axis_index("vocab") * (chunk * lax.axis_size("dp"))
    place = jnp.stack([first_row, y, x, core])
    cat = lambda *v: jnp.concatenate(v, axis=0)
    a = lambda dy, dx, lo, size: (dy, dx, lo, size)
    b = lambda dy, dx, lo, size: (dy, dx, h + lo, size)

    own = head_weight
    left, right = shift(own, 0, 1), shift(own, 0, -1)
    down, up = shift(own, 1, 0), shift(own, -1, 0)
    tokens = normalize(hidden_states, norm_gain)
    others = swap_cores(tokens)
    goals = cat(target_ids, swap_cores(target_ids)).reshape(2 * mine, 1, BLOCK)

    f_xp = shift(cat(down[h : h + q], up[h : h + q], left[:q], left[h : h + q]), 0, 1)
    f_xm = shift(cat(down[h + q :], up[h + q :], right[q:h], right[h + q :]), 0, -1)
    f_yp = shift(cat(left[:q], right[:q], down[h : h + q], down[:q]), 1, 0)
    f_ym = shift(cat(left[q:h], right[q:h], up[h + q :], up[q:h]), -1, 0)
    g_xp = shift(cat(down[h + q :], up[h + q :]), 0, 1)
    g_xm = shift(cat(down[h : h + q], up[h : h + q]), 0, -1)
    g_yp = shift(cat(left[q:h], right[q:h]), 1, 0)
    g_ym = shift(cat(left[:q], right[:q]), -1, 0)
    initial = cat(jnp.full((1, 1), lowest, jnp.float32), jnp.zeros((3, 1), jnp.float32))
    initial = jnp.broadcast_to(initial, (2 * mine, 4, BLOCK))
    fold_in = functools.partial(score, place, goals, own=tokens, other=others, chunk=chunk)
    whole = lambda dy, dx: [(dy, dx, 0, chunk)]
    (stats,) = fold_in(
        initial,
        pieces=[
            (own, whole(0, 0)),
            (left, whole(0, -1)),
            (right, whole(0, 1)),
            (down, whole(-1, 0)),
            (up, whole(1, 0)),
        ],
    )

    a2_low, a2_high = f_xp[2 * q : 3 * q], f_xm[2 * q : 3 * q]
    b2_low, b2_high = f_yp[2 * q : 3 * q], f_ym[2 * q : 3 * q]
    p_yp, p_ym = shift(a2_low, 1, 0), shift(a2_high, -1, 0)
    p_xp, p_xm = shift(b2_low, 0, 1), shift(b2_high, 0, -1)
    q_yp = shift(cat(a2_high, f_yp[: 2 * q]), 1, 0)
    q_ym = shift(cat(a2_low, f_ym[: 2 * q]), -1, 0)
    q_xp = shift(cat(b2_high, f_xp[: 2 * q]), 0, 1)
    q_xm = shift(cat(b2_low, f_xm[: 2 * q]), 0, -1)
    r_yp, r_ym = shift(p_yp, 1, 0), shift(p_ym, -1, 0)
    r_xp, r_xm = shift(p_xp, 0, 1), shift(p_xm, 0, -1)
    (stats,) = fold_in(
        stats,
        pieces=[
            (f_xp, [b(-1, -1, 0, q), b(1, -1, 0, q), a(0, 2, 0, q), b(0, 2, 0, q)]),
            (f_xm, [b(-1, 1, q, q), b(1, 1, q, q), a(0, 2, q, q), b(0, 2, q, q)]),
            (f_yp, [a(-1, -1, 0, q), a(-1, 1, 0, q), b(2, 0, 0, q), a(2, 0, 0, q)]),
            (f_ym, [a(1, -1, q, q), a(1, 1, q, q), b(2, 0, q, q), a(2, 0, q, q)]),
            (g_xp, [b(-1, -1, q, q), b(1, -1, q, q)]),
            (g_xm, [b(-1, 1, 0, q), b(1, 1, 0, q)]),
            (g_yp, [a(-1, -1, q, q), a(-1, 1, q, q)]),
            (g_ym, [a(1, -1, 0, q), a(1, 1, 0, q)]),
            (p_yp, [a(-1, 2, 0, q)]),
            (p_ym, [a(1, 2, q, q)]),
            (p_xp, [b(2, -1, 0, q)]),
            (p_xm, [b(2, 1, q, q)]),
        ],
    )
    ours, theirs = fold_in(
        stats,
        pieces=[
            (q_yp, [a(-1, 2, q, q), a(2, -1, 0, q), a(2, 1, 0, q)]),
            (q_ym, [a(1, 2, 0, q), a(2, -1, q, q), a(2, 1, q, q)]),
            (q_xp, [b(2, -1, q, q), b(-1, 2, 0, q), b(1, 2, 0, q)]),
            (q_xm, [b(2, 1, 0, q), b(-1, 2, q, q), b(1, 2, q, q)]),
            (r_yp, [a(2, 2, 0, q)]),
            (r_ym, [a(2, 2, q, q)]),
            (r_xp, [b(2, 2, 0, q)]),
            (r_xm, [b(2, 2, q, q)]),
        ],
        last=True,
    )

    ours = merge(ours, swap_cores(theirs))
    depth = lax.axis_size("vocab")
    forth = [(i, (i + 1) % depth) for i in range(depth)]
    back = [(i, (i - 1) % depth) for i in range(depth)]
    parts = [ours]
    rising = falling = ours
    for step in range(depth // 2):
        rising = lax.ppermute(rising, "vocab", forth)
        parts.append(rising)
        if step < depth // 2 - 1:
            falling = lax.ppermute(falling, "vocab", back)
            parts.append(falling)
    log_probs, entropies = finish(lengths, parts)
    return (log_probs.reshape(row_count), entropies.reshape(row_count))


def solution(mesh):
    in_specs = (P("dp", None), P(), P(("vocab", "dp"), None), P("dp"), P("dp"))
    out_specs = (P("dp"), P("dp"))
    return jax.shard_map(on_device, mesh=mesh, in_specs=in_specs, out_specs=out_specs, check_vma=False)
```
